1024 devices in a mesh: pipe: 8 (over z), dp: 32 (over x, y_hi), tensor: 4 (over y_lo, core).
Axes of the slice: x: 8, y: 8 (y_hi: 4, y_lo: 2; y = y_hi * 2 + y_lo), z: 8, core: 2. Of those that a mesh axis runs over, the one named last changes fastest.
Arguments:
- queries: bfloat16 [8, 4096, 8192], P('pipe', 'dp', 'tensor'), may hold values from -5.5 to 5.5
- cache_keys: bfloat16 [4096, 4, 8, 256], P('dp', 'tensor', 'pipe'), may hold values from -5.5 to 5.5
- cache_values: bfloat16 [4096, 4, 8, 256], P('dp', 'tensor', 'pipe'), may hold values from -40 to 40
- doc_lengths: int32 [32, 6], P('dp'), may hold values from 1 to 64, 128 in all within a row
- row_counts: int32 [32, 32], replicated, may hold values from 3 to 5, as said below
- out_gain: bfloat16 [8192], P('tensor'), may hold values from 0.099609375 to 1.8984375
Outputs:
- regrouped: bfloat16 [8, 4096, 8192], P('pipe', 'dp', 'tensor')
The draws below stay inside these ranges and needn't reach their ends.
Inputs may be any that keep to these rules, and one draw needn't show every extreme that they name: row_counts[i, j] is how many rows data group i sends to data group j; each row and each column of row_counts sums to 128; some entry equals 5 in every draw.
All inputs are finite; a program needn't handle non-finite values.
Results may differ from the reference program's by a relative error of at most 0.0085.
Values may be sent and summed in bfloat16 or wider, within the bound.
A program may use at most 32 MiB of HBM per device.

```python
import math
import jax
import jax.numpy as jnp
import numpy as np
from jax import lax

HEADS = 64
HEAD_DIM = 128
SEQ = 128
NDOC = 6
MOST = 64
TOKENS = 4096
N_PIPE = 8
N_DP = 32
N_TENSOR = 4


def shared_keys(key):
    base = jax.random.normal(jax.random.fold_in(key, 11), (TOKENS, HEADS * HEAD_DIM), jnp.float32)
    base = jnp.clip(base, -5.5, 5.5)
    return base


def draw_cache_keys(key, part):
    return shared_keys(key).reshape(TOKENS, N_TENSOR, N_PIPE, HEADS * HEAD_DIM // (N_TENSOR * N_PIPE)).astype(jnp.bfloat16)


def draw_queries(key, part):
    query = jax.random.normal(jax.random.fold_in(key, 13), (N_PIPE, TOKENS, HEADS * HEAD_DIM), jnp.float32)
    query = jnp.clip(query, -5.5, 5.5)
    return query.astype(jnp.bfloat16)


def draw_cache_values(key, part):
    values = jax.random.normal(jax.random.fold_in(key, 21), (TOKENS, HEADS, HEAD_DIM), jnp.float32)
    values = jnp.clip(values, -4.0, 4.0)
    spread = jax.random.uniform(jax.random.fold_in(key, 22), (HEADS,), jnp.float32)
    head_scale = 10.0 ** (0.5 * jnp.arange(HEADS, dtype=jnp.float32) / (HEADS - 1) + 0.5 * spread)
    row_scale = 10.0 ** jax.random.uniform(jax.random.fold_in(key, 23), (TOKENS,), jnp.float32)
    values = values * head_scale[None, :, None] * row_scale[:, None, None] / 10.0
    return values.reshape(TOKENS, N_TENSOR, N_PIPE, HEADS * HEAD_DIM // (N_TENSOR * N_PIPE)).astype(jnp.bfloat16)


def draw_row_counts(key, part):
    base = SEQ // N_DP
    quarter = base // 4
    offsets = jax.random.randint(jax.random.fold_in(key, 31), (N_DP // 2,), 0, quarter + 1)
    offsets = offsets.at[0].set(quarter)
    loads = jnp.stack([base + offsets, base - offsets], axis=1).reshape(N_DP)
    order = jax.random.permutation(jax.random.fold_in(key, 32), N_DP)
    loads = loads[order]
    rows = jnp.arange(N_DP)[:, None]
    cols = jnp.arange(N_DP)[None, :]
    return loads[(cols - rows) % N_DP].astype(jnp.int32)


def profile(number_of, total, reach, lean):
    weights = [(1 << 20) // math.isqrt(rank ** lean) + 1 for rank in range(2, number_of + 1)]
    spare, counts = total - reach - (number_of - 1), [1] * (number_of - 1)
    while spare > 0:
        movable = [i for i in range(number_of - 1) if counts[i] < reach]
        whole, budget = sum([weights[i] for i in movable]), spare
        for i in movable:
            extra = min(reach - counts[i], max(1, budget * weights[i] // whole), spare)
            counts[i] = counts[i] + extra
            spare = spare - extra
    return np.array([reach] + counts)


def ragged_sizes(stream_key, count, total, reach, skew):
    if count == 2:
        one = jax.random.randint(stream_key, (), max(1, total - reach), min(reach, total - 1) + 1)
        return jnp.stack([one, total - one])
    sizes = jnp.asarray(profile(count, total, reach, skew), jnp.int32)
    couples = (count - 1) // 2
    source_of, receiver = sizes[1:1 + 2 * couples:2], sizes[2:2 + 2 * couples:2]
    margin = jnp.minimum(source_of - 1, reach - receiver)
    moved = jax.random.randint(jax.random.fold_in(stream_key, 1), (couples,), 0, 1 << 20) % (margin + 1)
    sizes = sizes.at[1:1 + 2 * couples:2].set(source_of - moved).at[2:2 + 2 * couples:2].set(receiver + moved)
    return sizes[jax.random.permutation(jax.random.fold_in(stream_key, 2), count)]


def setup_inputs(seed: int = 0) -> dict:
    arg_keys = jax.random.split(jax.random.key(seed), 7)
    queries = draw_queries(jax.random.fold_in(arg_keys[6], 71), 0)
    cache_keys = draw_cache_keys(jax.random.fold_in(arg_keys[6], 71), 0)
    cache_values = draw_cache_values(jax.random.fold_in(arg_keys[6], 71), 0)
    doc_lengths = jax.vmap(lambda own: ragged_sizes(own, NDOC, SEQ, MOST, 2))(jax.random.split(arg_keys[3], N_DP)).reshape((N_DP, NDOC)).astype(jnp.int32)
    row_counts = draw_row_counts(jax.random.fold_in(arg_keys[6], 71), 0)
    out_gain = jnp.clip(1.0 + 0.18 * jax.random.normal(arg_keys[5], (HEADS * HEAD_DIM,), jnp.float32), 0.099609375, 1.8984375).astype(jnp.bfloat16)
    return {"queries": queries, "cache_keys": cache_keys, "cache_values": cache_values, "doc_lengths": doc_lengths, "row_counts": row_counts, "out_gain": out_gain}


masked_fill = -1e+30
norm_eps = 1e-06

def doc_ids(lengths, positions):
    ends = jnp.cumsum(lengths).astype(jnp.int32)
    return lax.optimization_barrier(jnp.sum((positions[:, None] >= ends[None, :]).astype(jnp.int32), axis=1))

def regroup_table(row_counts):
    send_start = jnp.cumsum(row_counts, axis=1).astype(jnp.int32) - row_counts
    col_end = jnp.cumsum(row_counts, axis=0).astype(jnp.int32)
    recv_start = col_end - row_counts
    positions = jnp.arange(SEQ, dtype=jnp.int32)
    source = lax.optimization_barrier(jnp.sum((positions[None, :, None] >= col_end.T[:, None, :]).astype(jnp.int32), axis=2))
    onehot = (source[:, :, None] == jnp.arange(N_DP, dtype=jnp.int32)[None, None, :]).astype(jnp.int32)
    begin = lax.optimization_barrier(jnp.sum(onehot * (send_start.T - recv_start.T)[:, None, :], axis=2))
    return (source * SEQ + positions[None, :] + begin).astype(jnp.int32)

def reference(queries, cache_keys, cache_values, doc_lengths, row_counts, out_gain):
    width = HEADS * HEAD_DIM
    scale = 1.0 / HEAD_DIM ** 0.5
    positions = jnp.arange(SEQ, dtype=jnp.int32)
    gain = out_gain.astype(jnp.float32)
    table = regroup_table(row_counts).reshape(-1)
    flat_keys = cache_keys.reshape(TOKENS, width)
    flat_values = cache_values.reshape(TOKENS, width)

    def one_group(section, group):
        start = (group * SEQ).astype(jnp.int32)
        keys = lax.dynamic_slice_in_dim(flat_keys, start, SEQ, 0).astype(jnp.float32).reshape(SEQ, HEADS, HEAD_DIM)
        values = lax.dynamic_slice_in_dim(flat_values, start, SEQ, 0).astype(jnp.float32).reshape(SEQ, HEADS, HEAD_DIM)
        query = lax.dynamic_slice(queries, (section, start, jnp.int32(0)), (1, SEQ, width))[0]
        query = query.astype(jnp.float32).reshape(SEQ, HEADS, HEAD_DIM)
        docs = doc_ids(lax.dynamic_index_in_dim(doc_lengths, group, 0, keepdims=False), positions)
        allowed = (docs[:, None] == docs[None, :]) & (positions[None, :] <= positions[:, None])
        scores = jnp.einsum('qhd,khd->hqk', query, keys, precision=lax.Precision.HIGHEST) * scale
        scores = jnp.where(allowed[None], scores, masked_fill)
        top = lax.optimization_barrier(jnp.max(scores, axis=2))
        weights = jnp.where(allowed[None], jnp.exp(scores - top[:, :, None]), 0.0)
        total = lax.optimization_barrier(jnp.sum(weights, axis=2))
        rounded = lax.optimization_barrier(weights.astype(jnp.bfloat16)).astype(jnp.float32)
        accum = jnp.einsum('hqk,khd->hqd', rounded, values, precision=lax.Precision.HIGHEST)
        attn = (accum / total[:, :, None]).transpose(1, 0, 2).reshape(SEQ, width).astype(jnp.bfloat16)
        wide = attn.astype(jnp.float32)
        mean_sq = lax.optimization_barrier(jnp.sum(wide * wide, axis=1)) / width
        return (wide * lax.rsqrt(mean_sq + norm_eps)[:, None] * gain[None, :]).astype(jnp.bfloat16)

    def one_section(section):
        normed = lax.map(lambda group: one_group(section, group), jnp.arange(N_DP, dtype=jnp.int32))
        return jnp.take(normed.reshape(TOKENS, width), table, axis=0)
    return lax.map(one_section, jnp.arange(N_PIPE, dtype=jnp.int32))
```

```python
import functools

import jax
import jax.numpy as jnp
from jax import lax
from jax.experimental import pallas as pl
from jax.experimental.pallas import tpu as pltpu
from jax.sharding import PartitionSpec as P

HEADS = 64
HEAD_DIM = 128

masked_fill = -1e30
norm_eps = 1e-06
MESH = pl.DeviceIdType.MESH
BLOCKS_PER_GROUP = 2


def dot(a, b, contract, **options):
    return lax.dot_general(a, b, (contract, ((), ())), preferred_element_type=jnp.float32, **options)


def iota(shape, dim):
    return lax.broadcasted_iota(jnp.int32, shape, dim)


def kernel(
    sizes,
    queries,
    keys,
    values,
    doc_lengths,
    row_counts,
    out_gain,
    out,
    query,
    cache,
    shape_buf,
    outbox,
    inbox,
    rows_buf,
    result,
    sums,
    load_sem,
    key_send,
    key_recv,
    value_send,
    value_recv,
    row_send,
    row_recv,
    sum_send,
    sum_recv,
):
    n_pipe, n_dp, n_tensor, seq, cap, n_docs = sizes
    half = n_pipe // 2
    slots = n_dp * cap
    block_width = cache.shape[-1]
    heads_block = block_width // HEAD_DIM
    heads_group = BLOCKS_PER_GROUP * heads_block
    groups = n_pipe // BLOCKS_PER_GROUP
    y_size = 4 if n_dp >= 4 else n_dp
    x_size = n_dp // y_size
    pipe = lax.axis_index("pipe")
    me = lax.axis_index("dp")
    tensor = lax.axis_index("tensor")
    right = {"pipe": lax.rem(pipe + 1, n_pipe)}
    left = {"pipe": lax.rem(pipe + n_pipe - 1, n_pipe)}

    def length(offset, size):
        return min(offset, size - offset)

    offsets = sorted(
        ((dx, dy) for dx in range(x_size) for dy in range(y_size) if dx or dy),
        key=lambda o: -length(o[0], x_size) - 2 * length(o[1], y_size),
    )
    x = me // y_size
    y = lax.rem(me, y_size)
    partners = [
        lax.rem(x + dx, x_size) * y_size + lax.rem(y + dy, y_size) for dx, dy in offsets
    ]
    tensor_peers = [lax.rem(tensor + k, n_tensor) for k in range(1, n_tensor)]

    barrier = pltpu.get_barrier_semaphore()
    devices = [right, left]
    devices += [{"tensor": t} for t in tensor_peers]
    devices += [{"dp": j} for j in partners]
    for device in devices:
        pl.semaphore_signal(barrier, inc=1, device_id=device, device_id_type=MESH)
    loads = [
        pltpu.make_async_copy(keys, cache.at[0, 0], load_sem.at[0]),
        pltpu.make_async_copy(values, cache.at[0, 1], load_sem.at[1]),
        pltpu.make_async_copy(queries.at[0], query, load_sem.at[2]),
    ]
    for load in loads:
        load.start()

    row = iota((seq, seq), 0)
    col = iota((seq, seq), 1)
    end = jnp.int32(0)
    row_doc = jnp.zeros((seq, seq), jnp.int32)
    col_doc = jnp.zeros((seq, seq), jnp.int32)
    for k in range(n_docs):
        end = end + doc_lengths[0, k]
        row_doc = row_doc + (row >= end).astype(jnp.int32)
        col_doc = col_doc + (col >= end).astype(jnp.int32)
    allowed = (row_doc == col_doc) & (col <= row)

    counts = row_counts[...].astype(jnp.float32)
    group_row = iota((n_dp, n_dp), 0)
    group_col = iota((n_dp, n_dp), 1)
    own_counts = jnp.sum(jnp.where(group_row == me, counts, 0.0), axis=0, keepdims=True)
    slot_of = iota((slots, n_dp), 0)
    lane_of = iota((slots, n_dp), 1)
    starts_at = lane_of * cap
    before = (starts_at + cap <= slot_of).astype(jnp.float32)
    same = ((starts_at <= slot_of) & (slot_of < starts_at + cap)).astype(jnp.float32)
    slot_col = iota((slots, 1), 0).astype(jnp.float32)
    index = slot_col - cap * jnp.sum(before, axis=1, keepdims=True)
    token = iota((slots, seq), 1).astype(jnp.float32)

    send_count = jnp.sum(same * own_counts, axis=1, keepdims=True)
    send_start = jnp.sum(before * own_counts, axis=1, keepdims=True)
    pick = (token == send_start + index) & (index < send_count)
    pick = pick.astype(jnp.float32).astype(jnp.bfloat16)

    narrow = counts.astype(jnp.bfloat16)
    mine = lane_of == me
    contract = ((1,), (0,))
    recv_count = dot(same.astype(jnp.bfloat16), narrow, contract)
    recv_count = jnp.sum(jnp.where(mine, recv_count, 0.0), axis=1, keepdims=True)
    recv_start = dot(before.astype(jnp.bfloat16), narrow, contract)
    recv_start = jnp.sum(jnp.where(mine, recv_start, 0.0), axis=1, keepdims=True)
    place = (token == recv_start + index) & (index < recv_count)
    place = jnp.transpose(place.astype(jnp.float32)).astype(jnp.bfloat16)

    for load in loads[:2]:
        load.wait()
    pl.semaphore_wait(barrier, len(devices))

    def ring(slot, into, part, way, step):
        send, recv = (key_send, key_recv) if part == 0 else (value_send, value_recv)
        return pltpu.make_async_remote_copy(
            src_ref=cache.at[slot, part],
            dst_ref=cache.at[into, part],
            send_sem=send.at[way, step],
            recv_sem=recv.at[way, step],
            device_id=left if way else right,
            device_id_type=MESH,
        )

    hops = {}

    def forward(step):
        for part in (0, 1):
            for way in (0, 1):
                if step + 1 == half and part != way:
                    continue
                slot = 0 if step == 0 else 2 * step - 1 + way
                into = 2 * half - 1 if step + 1 == half else 2 * step + 1 + way
                hops[part, way, step] = ring(slot, into, part, way, step)
                hops[part, way, step].start()

    def arrive(step):
        for part in (0, 1):
            for way in (0, 1):
                if (part, way, step - 1) in hops:
                    hops[part, way, step - 1].wait_recv()

    def source(block):
        if block == 0:
            return pipe
        d = (block + 1) // 2
        return lax.rem(pipe + (d if block % 2 == 0 else n_pipe - d), n_pipe)

    scale = 1.0 / HEAD_DIM**0.5

    def attend(block):
        for h in range(heads_block):
            lanes = pl.ds(h * HEAD_DIM, HEAD_DIM)
            column = pl.multiple_of(source(block) * block_width + h * HEAD_DIM, HEAD_DIM)
            scores = dot(query[:, pl.ds(column, HEAD_DIM)], cache[block, 0, :, lanes], ((1,), (1,)))
            scores = jnp.where(allowed, scores * scale, masked_fill)
            top = jnp.max(scores, axis=1, keepdims=True)
            weights = jnp.where(allowed, jnp.exp(scores - top), 0.0)
            total = jnp.sum(weights, axis=1, keepdims=True)
            accum = dot(weights.astype(jnp.bfloat16), cache[block, 1, :, lanes], ((1,), (0,)))
            attn = (accum / total).astype(jnp.bfloat16)
            picked = dot(pick, attn, ((1,), (0,)))
            shape_buf[:, (block % BLOCKS_PER_GROUP) * heads_block + h, :] = picked

    def send_rows(group):
        outbox[group] = shape_buf[...].astype(jnp.bfloat16)
        mine = pl.ds(me * cap, cap)
        for j in partners:
            pltpu.make_async_remote_copy(
                src_ref=outbox.at[group, pl.ds(j * cap, cap)],
                dst_ref=inbox.at[group, mine],
                send_sem=row_send.at[group],
                recv_sem=row_recv.at[group],
                device_id={"dp": j},
                device_id_type=MESH,
            ).start()
        inbox[group, mine] = outbox[group, mine]

    def whole(group, sem):
        most = pl.ds(0, slots - cap)
        return pltpu.make_async_copy(outbox.at[group, most], inbox.at[group, most], sem.at[group])

    forward(0)
    loads[2].wait()
    arrived = 0
    for block in range(n_pipe):
        need = (block + 1) // 2
        if need > arrived:
            arrive(need)
            arrived = need
            if need < half:
                forward(need)
        attend(block)
        if (block + 1) % BLOCKS_PER_GROUP == 0:
            send_rows(block // BLOCKS_PER_GROUP)

    squares = jnp.zeros((seq, HEAD_DIM), jnp.float32)
    for group in range(groups):
        whole(group, row_recv).wait()
        rows_buf[...] = inbox[group].astype(jnp.float32)
        for h in range(heads_group):
            rows = dot(place, rows_buf[:, h, :].astype(jnp.bfloat16), ((1,), (0,)))
            result[group * heads_group + h] = rows
            squares = squares + rows * rows
    ones = jnp.ones((8, HEAD_DIM), jnp.float32)
    sums[0] = dot(ones, squares, ((1,), (1,)), precision=lax.Precision.HIGHEST)
    copies = []
    for k, t in enumerate(tensor_peers):
        copies.append(
            pltpu.make_async_remote_copy(
                src_ref=sums.at[0],
                dst_ref=sums.at[1 + k],
                send_sem=sum_send.at[k],
                recv_sem=sum_recv.at[k],
                device_id={"tensor": t},
                device_id_type=MESH,
            )
        )
        copies[-1].start()
    for copy in copies:
        copy.wait_recv()
    total = sums[0]
    for k in range(1, n_tensor):
        total = total + sums[k]
    total = jnp.broadcast_to(total[0:1], (seq, seq))
    factor = lax.rsqrt(jnp.transpose(total) / (HEADS * HEAD_DIM) + norm_eps)
    for block in range(n_pipe):
        for h in range(heads_block):
            lanes = pl.ds(pl.multiple_of(source(block) * block_width + h * HEAD_DIM, HEAD_DIM), HEAD_DIM)
            gain = out_gain[:, lanes].astype(jnp.float32)
            out[0, :, lanes] = (result[block * heads_block + h] * factor * gain).astype(jnp.bfloat16)

    for hop in hops.values():
        hop.wait_send()
    for group in range(groups):
        whole(group, row_send).wait()
    for copy in copies:
        copy.wait_send()


def body(queries, cache_keys, cache_values, doc_lengths, row_counts, out_gain):
    n_pipe, n_dp, n_tensor = (lax.axis_size(name) for name in ("pipe", "dp", "tensor"))
    seq, width = queries.shape[1:]
    block_width = cache_keys.shape[-1]
    cap = 5 * seq // (4 * n_dp)
    slots = n_dp * cap
    heads_group = BLOCKS_PER_GROUP * block_width // HEAD_DIM
    groups = n_pipe // BLOCKS_PER_GROUP
    half = n_pipe // 2
    sizes = (n_pipe, n_dp, n_tensor, seq, cap, doc_lengths.shape[1])
    vmem = pl.BlockSpec(memory_space=pltpu.VMEM)
    smem = pl.BlockSpec(memory_space=pltpu.SMEM)
    anywhere = pl.BlockSpec(memory_space=pl.ANY)
    dma = pltpu.SemaphoreType.DMA
    return pl.pallas_call(
        functools.partial(kernel, sizes),
        out_shape=jax.ShapeDtypeStruct(queries.shape, queries.dtype),
        in_specs=[anywhere, anywhere, anywhere, smem, vmem, vmem],
        out_specs=vmem,
        scratch_shapes=[
            pltpu.VMEM((seq, width), jnp.bfloat16),
            pltpu.VMEM((n_pipe, 2, seq, block_width), jnp.bfloat16),
            pltpu.VMEM((slots, heads_group, HEAD_DIM), jnp.float32),
            pltpu.VMEM((groups, slots, heads_group, HEAD_DIM), jnp.bfloat16),
            pltpu.VMEM((groups, slots, heads_group, HEAD_DIM), jnp.bfloat16),
            pltpu.VMEM((slots, heads_group, HEAD_DIM), jnp.float32),
            pltpu.VMEM((width // HEAD_DIM, seq, HEAD_DIM), jnp.float32),
            pltpu.VMEM((n_tensor, 8, HEAD_DIM), jnp.float32),
            dma((3,)),
            dma((2, half)),
            dma((2, half)),
            dma((2, half)),
            dma((2, half)),
            dma((groups,)),
            dma((groups,)),
            dma((n_tensor - 1,)),
            dma((n_tensor - 1,)),
        ],
        compiler_params=pltpu.CompilerParams(collective_id=0, has_side_effects=True),
        name="attend_regroup",
    )(
        queries,
        cache_keys.reshape(seq, block_width),
        cache_values.reshape(seq, block_width),
        doc_lengths,
        row_counts,
        out_gain.reshape(1, width),
    )


def solution(mesh):
    return jax.shard_map(
        body,
        mesh=mesh,
        in_specs=(
            P("pipe", "dp", "tensor"),
            P("dp", "tensor", "pipe", None),
            P("dp", "tensor", "pipe", None),
            P("dp", None),
            P(),
            P("tensor"),
        ),
        out_specs=P("pipe", "dp", "tensor"),
        check_vma=False,
    )
```

```python
import functools

import jax
import jax.numpy as jnp
from jax import lax
from jax.experimental import pallas as pl
from jax.experimental.pallas import tpu as pltpu
from jax.sharding import PartitionSpec as P

HEADS = 64
HEAD_DIM = 128

masked_fill = -1e30
norm_eps = 1e-06
MESH = pl.DeviceIdType.MESH
HEADS_PER_GROUP = 4


def dot(a, b, contract, **options):
    return lax.dot_general(a, b, (contract, ((), ())), preferred_element_type=jnp.float32, **options)


def iota(shape, dim):
    return lax.broadcasted_iota(jnp.int32, shape, dim)


def kernel(
    sizes,
    queries,
    keys,
    values,
    doc_lengths,
    row_counts,
    out,
    factor_out,
    query,
    cache,
    shape_buf,
    outbox,
    inbox,
    rows_buf,
    result,
    sums,
    load_sem,
    store_sem,
    hop_send,
    hop_recv,
    row_send,
    row_recv,
    sum_send,
    sum_recv,
):
    n_pipe, n_dp, n_tensor, seq, cap, n_docs = sizes
    half = n_pipe // 2
    slots = n_dp * cap
    heads_block = cache.shape[1]
    groups = n_pipe * heads_block // HEADS_PER_GROUP
    y_size = 4 if n_dp >= 4 else n_dp
    x_size = n_dp // y_size
    pipe = lax.axis_index("pipe")
    me = lax.axis_index("dp")
    tensor = lax.axis_index("tensor")
    right = {"pipe": lax.rem(pipe + 1, n_pipe)}
    left = {"pipe": lax.rem(pipe + n_pipe - 1, n_pipe)}

    def length(offset, size):
        return min(offset, size - offset)

    offsets = sorted(
        ((dx, dy) for dx in range(x_size) for dy in range(y_size) if dx or dy),
        key=lambda o: -length(o[0], x_size) - 2 * length(o[1], y_size),
    )
    x = me // y_size
    y = lax.rem(me, y_size)
    partners = [
        lax.rem(x + dx, x_size) * y_size + lax.rem(y + dy, y_size) for dx, dy in offsets
    ]
    tensor_peers = [lax.rem(tensor + k, n_tensor) for k in range(1, n_tensor)]

    barrier = pltpu.get_barrier_semaphore()
    devices = [right, left]
    devices += [{"tensor": t} for t in tensor_peers]
    devices += [{"dp": j} for j in partners]
    for device in devices:
        pl.semaphore_signal(barrier, inc=1, device_id=device, device_id_type=MESH)
    loads = [
        pltpu.make_async_copy(
            array.at[:, pl.ds(h * HEAD_DIM, HEAD_DIM)], cache.at[0, h, part], load_sem.at[h, part]
        )
        for h in range(heads_block)
        for part, array in enumerate((keys, values))
    ]
    loads.append(pltpu.make_async_copy(queries.at[0], query, load_sem.at[heads_block, 0]))
    for load in loads:
        load.start()

    for load in loads[:-1]:
        load.wait()
    pl.semaphore_wait(barrier, len(devices))

    hops = {}

    def order(way):
        return range(heads_block) if way == 0 else range(heads_block - 1, -1, -1)

    def forward(step, way, h, part):
        last = step + 1 == half
        slot = 0 if step == 0 else 2 * step - 1 + way
        into = 2 * half - 1 if last else 2 * step + 1 + way
        copy = pltpu.make_async_remote_copy(
            src_ref=cache.at[slot, h, part],
            dst_ref=cache.at[into, h, part],
            send_sem=hop_send.at[step, way, h, part],
            recv_sem=hop_recv.at[step, way, h, part],
            device_id=left if way else right,
            device_id_type=MESH,
        )
        copy.start()
        hops[step + 1, way, h, part] = copy

    for i in range(heads_block):
        for part in (0, 1):
            for way in (0, 1):
                forward(0, way, order(way)[i], part)

    row = iota((seq, seq), 0)
    col = iota((seq, seq), 1)
    end = jnp.int32(0)
    row_doc = jnp.zeros((seq, seq), jnp.int32)
    col_doc = jnp.zeros((seq, seq), jnp.int32)
    for k in range(n_docs):
        end = end + doc_lengths[0, k]
        row_doc = row_doc + (row >= end).astype(jnp.int32)
        col_doc = col_doc + (col >= end).astype(jnp.int32)
    allowed = (row_doc == col_doc) & (col <= row)

    counts = row_counts[...].astype(jnp.float32)
    group_row = iota((n_dp, n_dp), 0)
    group_col = iota((n_dp, n_dp), 1)
    own_counts = jnp.sum(jnp.where(group_row == me, counts, 0.0), axis=0, keepdims=True)
    slot_of = iota((slots, n_dp), 0)
    lane_of = iota((slots, n_dp), 1)
    starts_at = lane_of * cap
    before = (starts_at + cap <= slot_of).astype(jnp.float32)
    same = ((starts_at <= slot_of) & (slot_of < starts_at + cap)).astype(jnp.float32)
    slot_col = iota((slots, 1), 0).astype(jnp.float32)
    index = slot_col - cap * jnp.sum(before, axis=1, keepdims=True)
    token = iota((slots, seq), 1).astype(jnp.float32)

    send_count = jnp.sum(same * own_counts, axis=1, keepdims=True)
    send_start = jnp.sum(before * own_counts, axis=1, keepdims=True)
    pick = (token == send_start + index) & (index < send_count)
    pick = pick.astype(jnp.float32).astype(jnp.bfloat16)

    narrow = counts.astype(jnp.bfloat16)
    mine = lane_of == me
    contract = ((1,), (0,))
    recv_count = dot(same.astype(jnp.bfloat16), narrow, contract)
    recv_count = jnp.sum(jnp.where(mine, recv_count, 0.0), axis=1, keepdims=True)
    recv_start = dot(before.astype(jnp.bfloat16), narrow, contract)
    recv_start = jnp.sum(jnp.where(mine, recv_start, 0.0), axis=1, keepdims=True)
    place = (token == recv_start + index) & (index < recv_count)
    place = jnp.transpose(place.astype(jnp.float32)).astype(jnp.bfloat16)

    def column(block, h):
        d = (block + 1) // 2
        z = lax.rem(pipe + (d if block % 2 == 0 else n_pipe - d), n_pipe)
        return pl.ds(pl.multiple_of((z * heads_block + h) * HEAD_DIM, HEAD_DIM), HEAD_DIM)

    scale = 1.0 / HEAD_DIM**0.5
    done = []

    def attend(block, h):
        scores = dot(query[:, column(block, h)], cache[block, h, 0], ((1,), (1,)))
        scores = jnp.where(allowed, scores * scale, masked_fill)
        top = jnp.max(scores, axis=1, keepdims=True)
        weights = jnp.where(allowed, jnp.exp(scores - top), 0.0)
        total = jnp.sum(weights, axis=1, keepdims=True)
        accum = dot(weights.astype(jnp.bfloat16), cache[block, h, 1], contract)
        attn = (accum / total).astype(jnp.bfloat16)
        shape_buf[:, len(done) % HEADS_PER_GROUP, :] = dot(pick, attn, contract)
        done.append((block, h))
        if len(done) % HEADS_PER_GROUP == 0:
            send_rows(len(done) // HEADS_PER_GROUP - 1)

    def send_rows(group):
        outbox[group] = shape_buf[...].astype(jnp.bfloat16)
        mine = pl.ds(me * cap, cap)
        for j in partners:
            pltpu.make_async_remote_copy(
                src_ref=outbox.at[group, pl.ds(j * cap, cap)],
                dst_ref=inbox.at[group, mine],
                send_sem=row_send.at[group],
                recv_sem=row_recv.at[group],
                device_id={"dp": j},
                device_id_type=MESH,
            ).start()
        inbox[group, mine] = outbox[group, mine]

    def whole(group, sem):
        most = pl.ds(0, slots - cap)
        return pltpu.make_async_copy(outbox.at[group, most], inbox.at[group, most], sem.at[group])

    loads[-1].wait()
    for h in range(heads_block):
        attend(0, h)
    for step in range(1, half + 1):
        for i in range(heads_block // 2 if step == half else heads_block):
            for part in (0, 1):
                for way in (0, 1):
                    h = order(way)[i]
                    hops[step, way, h, part].wait_recv()
                    if step + 1 < half or (step + 1 == half and i < heads_block // 2):
                        forward(step, way, h, part)
            for way in (0, 1):
                attend(2 * step - 1 if step == half else 2 * step - 1 + way, order(way)[i])

    squares = jnp.zeros((seq, HEAD_DIM), jnp.float32)
    stores = []
    for group in range(groups):
        whole(group, row_recv).wait()
        rows_buf[...] = inbox[group].astype(jnp.float32)
        for i in range(HEADS_PER_GROUP):
            n = group * HEADS_PER_GROUP + i
            rows = dot(place, rows_buf[:, i, :].astype(jnp.bfloat16), contract)
            squares = squares + rows * rows
            result[n] = rows.astype(jnp.bfloat16)
            stores.append(
                pltpu.make_async_copy(result.at[n], out.at[:, column(*done[n])], store_sem.at[n])
            )
            stores[-1].start()
    ones = jnp.ones((8, HEAD_DIM), jnp.float32)
    sums[0] = dot(ones, squares, ((1,), (1,)), precision=lax.Precision.HIGHEST)
    copies = []
    for k, t in enumerate(tensor_peers):
        copies.append(
            pltpu.make_async_remote_copy(
                src_ref=sums.at[0],
                dst_ref=sums.at[1 + k],
                send_sem=sum_send.at[k],
                recv_sem=sum_recv.at[k],
                device_id={"tensor": t},
                device_id_type=MESH,
            )
        )
        copies[-1].start()
    for hop in hops.values():
        hop.wait_send()
    for group in range(groups):
        whole(group, row_send).wait()
    for store in stores:
        store.wait()
    for copy in copies:
        copy.wait()
    total = sums[0]
    for k in range(1, n_tensor):
        total = total + sums[k]
    total = jnp.transpose(jnp.broadcast_to(total[0:1], (seq, seq)))
    factor_out[...] = lax.rsqrt(total / (HEADS * HEAD_DIM) + norm_eps)


def body(queries, cache_keys, cache_values, doc_lengths, row_counts, out_gain):
    n_pipe, n_dp, n_tensor = (lax.axis_size(name) for name in ("pipe", "dp", "tensor"))
    seq, width = queries.shape[1:]
    block_width = cache_keys.shape[-1]
    heads_block = block_width // HEAD_DIM
    heads = width // HEAD_DIM
    cap = 5 * seq // (4 * n_dp)
    slots = n_dp * cap
    groups = heads // HEADS_PER_GROUP
    half = n_pipe // 2
    sizes = (n_pipe, n_dp, n_tensor, seq, cap, doc_lengths.shape[1])
    vmem = pl.BlockSpec(memory_space=pltpu.VMEM)
    smem = pl.BlockSpec(memory_space=pltpu.SMEM)
    anywhere = pl.BlockSpec(memory_space=pl.ANY)
    dma = pltpu.SemaphoreType.DMA
    rows, factor = pl.pallas_call(
        functools.partial(kernel, sizes),
        out_shape=(
            jax.ShapeDtypeStruct((seq, width), jnp.bfloat16),
            jax.ShapeDtypeStruct((seq, seq), jnp.float32),
        ),
        in_specs=[anywhere, anywhere, anywhere, smem, vmem],
        out_specs=(anywhere, vmem),
        scratch_shapes=[
            pltpu.VMEM((seq, width), jnp.bfloat16),
            pltpu.VMEM((n_pipe, heads_block, 2, seq, HEAD_DIM), jnp.bfloat16),
            pltpu.VMEM((slots, HEADS_PER_GROUP, HEAD_DIM), jnp.float32),
            pltpu.VMEM((groups, slots, HEADS_PER_GROUP, HEAD_DIM), jnp.bfloat16),
            pltpu.VMEM((groups, slots, HEADS_PER_GROUP, HEAD_DIM), jnp.bfloat16),
            pltpu.VMEM((slots, HEADS_PER_GROUP, HEAD_DIM), jnp.float32),
            pltpu.VMEM((heads, seq, HEAD_DIM), jnp.bfloat16),
            pltpu.VMEM((n_tensor, 8, HEAD_DIM), jnp.float32),
            dma((heads_block + 1, 2)),
            dma((heads,)),
            dma((half, 2, heads_block, 2)),
            dma((half, 2, heads_block, 2)),
            dma((groups,)),
            dma((groups,)),
            dma((n_tensor - 1,)),
            dma((n_tensor - 1,)),
        ],
        compiler_params=pltpu.CompilerParams(collective_id=0, has_side_effects=True),
        name="attend_regroup",
    )(
        queries,
        cache_keys.reshape(seq, block_width),
        cache_values.reshape(seq, block_width),
        doc_lengths,
        row_counts,
    )
    normed = rows.astype(jnp.float32) * factor[:, :1] * out_gain.astype(jnp.float32)[None, :]
    return normed.astype(jnp.bfloat16)[None]


def solution(mesh):
    return jax.shard_map(
        body,
        mesh=mesh,
        in_specs=(
            P("pipe", "dp", "tensor"),
            P("dp", "tensor", "pipe", None),
            P("dp", "tensor", "pipe", None),
            P("dp", None),
            P(),
            P("tensor"),
        ),
        out_specs=P("pipe", "dp", "tensor"),
        check_vma=False,
    )
```
